32 devices in a mesh: tok: 8 (over y, x, core), col: 4 (over z).
Axes of the slice: x: 2, y: 2, z: 4, core: 2. Of those that a mesh axis runs over, the one named last changes fastest.
Arguments:
- activations: bfloat16 [2, 12288, 4096], P(None, 'tok', 'col'), may hold values from -6 to 6
- out_grads: bfloat16 [2, 12288, 4096], P(None, 'tok', 'col'), may hold values from -0.059814453 to 0.059814453
- token_mask: int32 [2, 12288], P(None, 'tok'), may hold values 0 or 1
- row_signs: int32 [4096], P('tok'), may hold values from 0 to 1
- col_signs: int32 [4096], P('col'), may hold values from 0 to 1
- bank: float32 [16, 4096, 4096], P(None, 'tok', 'col'), may hold values from -6 to 6
- bank_index: int32 [2], replicated, may hold values from 0 to 15, as said below
Outputs:
- fingerprints: float32 [2, 4096, 4096], P(None, 'tok', 'col')
- scores: float32 [2], replicated
The draws below stay inside these ranges and needn't reach their ends.
Inputs may be any that keep to these rules, and one draw needn't show every extreme that they name: `bank_index`: the 2 values are distinct, and one of them is 15.
All inputs are finite; a program needn't handle non-finite values. No bound on the sum of `token_mask` on one device may be relied on, other than what follows from the above.
Results may differ from the reference program's by a relative error of at most 0.0003.
Values may be sent and summed in bfloat16 or wider, within the bound.
No kernel may reach another device: no remote copies, remote signals or barrier semaphores. Data moves between devices by JAX's collectives and lax.ppermute only.
A program may use at most 192 MiB of HBM per device.

```python
import math
import jax
import jax.numpy as jnp
from jax import lax

D = 4096
SEQS = 2
BANK = 16
TOKENS = 12288


def draw_bank_index(key, part):
    order = jax.random.permutation(jax.random.fold_in(key, 7), BANK - 1)[:SEQS].astype(jnp.int32)
    position = jax.random.randint(jax.random.fold_in(key, 11), (), 0, SEQS)
    slots = jnp.arange(SEQS, dtype=jnp.int32)
    return jnp.where(slots == position, BANK - 1, order).astype(jnp.int32)


def place_ends(array, own_key, smallest, top_value):
    extent = array.shape
    spot = [jax.random.randint(jax.random.fold_in(own_key, axis), (), 0, extent[axis]) for axis in range(len(extent))]
    array = array.at[tuple(spot)].set(smallest)
    longest = extent.index(max(extent))
    spot[longest] = (spot[longest] + 1) % extent[longest]
    return array.at[tuple(spot)].set(top_value)


def shard_levels(rng, shape, pieces, least, top_value):
    level = 1.0
    for dim, shards_of in pieces:
        draws = jax.random.uniform(jax.random.fold_in(jax.random.fold_in(rng, 6), dim), (shards_of,), jnp.float32, least / len(pieces), top_value / len(pieces))
        level = level * jnp.repeat(jnp.exp(draws), shape[dim] // shards_of).reshape((-1,) + (1,) * (len(shape) - 1 - dim))
    return level


def noise(key, extent, scale, reach, pieces=(), kind=jnp.bfloat16):
    result = scale * jax.random.normal(key, extent, jnp.float32)
    if pieces:
        result = result * shard_levels(key, extent, pieces, -0.22, 0.18)
    return jnp.clip(result, -reach, reach).astype(kind)


def setup_inputs(seed: int = 0) -> dict:
    key_of = jax.random.split(jax.random.key(seed), 8)
    return {
        "activations": noise(key_of[0], (SEQS, TOKENS, D), 1.0, 6.0, ((1, 8), (2, 4))),
        "out_grads": noise(key_of[1], (SEQS, TOKENS, D), 0.01, 0.059814453, ((1, 8), (2, 4))),
        "token_mask": place_ends((jax.random.randint(key_of[2], (SEQS, TOKENS), 0, 4) < 3).astype(jnp.int32), jax.random.fold_in(key_of[2], 1), 0, 1),
        "row_signs": place_ends(jax.random.randint(key_of[3], (D,), 0, 2), jax.random.fold_in(key_of[3], 1), 0, 1).astype(jnp.int32),
        "col_signs": place_ends(jax.random.randint(key_of[4], (D,), 0, 2), jax.random.fold_in(key_of[4], 1), 0, 1).astype(jnp.int32),
        "bank": noise(key_of[5], (BANK, D, D), 1.0, 6.0, ((1, 8), (2, 4)), jnp.float32),
        "bank_index": draw_bank_index(jax.random.fold_in(key_of[7], 71), 0),
    }


HIGH = lax.Precision.HIGHEST

def hadamard(order):
    positions = jnp.arange(order, dtype=jnp.int32)
    common_bits = jnp.bitwise_and(positions[:, None], positions[None, :])
    parity = jnp.zeros((order, order), jnp.int32)
    for bit_number in range(max(order.bit_length() - 1, 0)):
        parity = parity + jnp.bitwise_and(jnp.right_shift(common_bits, bit_number), 1)
    return (1 - 2 * (parity % 2)).astype(jnp.float32)

def mix_rows(matrix):
    first = 2 ** ((D.bit_length() - 1) // 2)
    second = D // first
    blocks = matrix.reshape(first, second, matrix.shape[1])
    blocks = jnp.einsum('ab,bqm->aqm', hadamard(first), blocks, precision=HIGH)
    blocks = jnp.einsum('qr,arm->aqm', hadamard(second), blocks, precision=HIGH)
    return blocks.reshape(D, matrix.shape[1]) / math.sqrt(D)

def reference(activations, out_grads, token_mask, row_signs, col_signs, bank, bank_index):
    row_pm = (2 * row_signs - 1).astype(jnp.float32)
    col_pm = (2 * col_signs - 1).astype(jnp.float32)
    prints = []
    scores = []
    squared = float(D) * float(D)
    for seq_number in range(SEQS):
        masked = out_grads[seq_number] * token_mask[seq_number][:, None].astype(jnp.bfloat16)
        gradient = jnp.dot(activations[seq_number].T, masked, preferred_element_type=jnp.float32)
        signed = gradient * row_pm[:, None] * col_pm[None, :]
        rows_done = mix_rows(signed)
        finished = mix_rows(rows_done.T).T
        chosen = lax.dynamic_index_in_dim(bank, bank_index[seq_number], 0, keepdims=False)
        cross = jnp.sum(finished * chosen)
        own = jnp.sum(finished * finished)
        refsq = jnp.sum(chosen * chosen)
        score = D * (cross / squared) / jnp.sqrt((own / squared + 1e-06) * (refsq / squared + 1e-06))
        prints.append(finished)
        scores.append(score)
    return (jnp.stack(prints), jnp.stack(scores))
```

```python
import math

import jax
import jax.numpy as jnp
from jax import lax
from jax.sharding import PartitionSpec as P


F32 = jnp.float32
BF16 = jnp.bfloat16


def bits_of(size):
    assert size & (size - 1) == 0
    return size.bit_length() - 1


def hadamard(order):
    positions = jnp.arange(order, dtype=jnp.int32)
    common_bits = jnp.bitwise_and(positions[:, None], positions[None, :])
    parity = jnp.zeros((order, order), jnp.int32)
    for bit_number in range(bits_of(order)):
        parity = parity + jnp.bitwise_and(jnp.right_shift(common_bits, bit_number), 1)
    return (1 - 2 * (parity % 2)).astype(BF16)


def swap(value, axis, distance):
    size = lax.axis_size(axis)
    return lax.ppermute(value, axis, [(i, i ^ distance) for i in range(size)])


def sign_of(bit):
    return (1 - 2 * bit).astype(F32)


class Place:
    def __init__(self, width, rows, cols):
        self.tok_bits = bits_of(lax.axis_size("tok"))
        self.col_bits = bits_of(lax.axis_size("col"))
        assert self.tok_bits >= self.col_bits >= 2
        self.extra = self.tok_bits - self.col_bits
        self.others = self.col_bits - 1
        tok, col = lax.axis_index("tok"), lax.axis_index("col")
        self.tok = [(tok >> k) & 1 for k in range(self.tok_bits)]
        self.col = [(col >> k) & 1 for k in range(self.col_bits)]
        self.width, self.rows, self.cols = width, rows, cols
        self.fine = rows >> self.others


def scatter_rows(place, parts, signs, y_first):
    width = parts[0].shape[1]
    block = (2,) * place.extra + (1 << place.others, place.fine, width)
    value = jnp.stack([(g * r[:, None]).reshape(block) for g, r in zip(parts, signs)])
    for step in range(place.extra):
        tok_bit = place.extra - 1 - step
        mine = sign_of(place.tok[tok_bit])
        first, second = value[:, 0], value[:, 1]
        value = first + mine * second + swap(first - mine * second, "tok", 1 << tok_bit)

    def pair_stage(value):
        tok_bit = place.extra
        bit = place.tok[tok_bit]
        s = sign_of(place.col[0])
        bit_f = bit.astype(F32)
        keep = 1 - bit_f + bit_f * s
        send = bit_f + (1 - bit_f) * s
        keep_2 = 1 - bit_f - bit_f * s
        send_2 = bit_f - (1 - bit_f) * s
        got = swap(send * value[0] + send_2 * value[1], "tok", 1 << tok_bit)
        return keep * value[0] + keep_2 * value[1] + got

    def held_stage(value):
        for k in range(1, place.col_bits):
            tok_bit = place.extra + k
            bit = place.tok[tok_bit]
            axis = value.ndim - 3
            halves = value.reshape(value.shape[:axis] + (value.shape[axis] // 2, 2) + value.shape[axis + 1:])
            keep = lax.dynamic_index_in_dim(halves, bit, axis + 1, keepdims=False)
            send = lax.dynamic_index_in_dim(halves, 1 - bit, axis + 1, keepdims=False)
            value = keep + swap(send, "tok", 1 << tok_bit)
        return value

    value = pair_stage(held_stage(value)) if y_first else held_stage(pair_stage(value))
    return value.reshape(place.fine, width)


def mix_low_col(place, slab):
    return sign_of(place.col[0]) * slab + swap(slab, "col", 1)


def mix_over_col(place, slabs):
    values = list(slabs)
    for k in range(1, place.col_bits):
        s = sign_of(place.col[k])
        mixed = []
        for base in range(0, len(values), 2):
            first, second = values[base], values[base + 1]
            keep = s * first + second
            send = first - s * second
            got = swap(send, "col", 1 << k)
            mixed.append(jnp.stack([keep + got, s * (keep - got)]))
        values = mixed
    value = values[0]
    for index in range(place.others):
        k = place.col_bits - 1 - index
        tok_bit = place.extra + k
        bit = place.tok[tok_bit]
        keep = lax.dynamic_index_in_dim(value, bit, index, keepdims=True)
        send = lax.dynamic_index_in_dim(value, 1 - bit, index, keepdims=True)
        got = swap(send, "tok", 1 << tok_bit)
        value = jnp.concatenate([keep, got], axis=index)
    return value


def pipeline(place, feats, masked, row_pm, chunks):
    block = feats[0].shape[1]
    col = lax.axis_index("col")
    signs = [
        lax.dynamic_slice_in_dim(row_pm, (col ^ other) * block, block) for other in (0, 1)
    ]
    result = []
    for seq_number, (a, m) in enumerate(zip(feats, masked)):
        count = chunks[seq_number]
        width = block // count
        a_pair = [a, swap(a, "col", 1)]
        pieces = [m[:, c * width:(c + 1) * width] for c in range(count)]
        column_sets = [[p] for p in pieces]
        for k in range(1, place.col_bits):
            for c in range(count):
                have = column_sets[c]
                column_sets[c] = have + [swap(p, "col", 1 << k) for p in have]
        done = []
        for c in range(count):
            slabs = []
            for number, p in enumerate(column_sets[c]):
                parts = [
                    lax.dot_general(x, p, (((0,), (0,)), ((), ())), preferred_element_type=F32)
                    for x in a_pair
                ]
                slab = scatter_rows(place, parts, signs, (number + c) % 2 == 1)
                slabs.append(mix_low_col(place, slab))
            done.append(mix_over_col(place, slabs))
        result.append(jnp.concatenate(done, axis=-1))
    return result


def exact_pieces(value):
    high = lax.reduce_precision(value, 8, 7)
    return high.astype(BF16), (value - high).astype(BF16)


def times_table(value, table, left):
    high, low = exact_pieces(value)
    if left:
        return sum(jnp.einsum("qr,arm->aqm", table, v, preferred_element_type=F32) for v in (high, low))
    return sum(jnp.einsum("arm,mc->arc", v, table, preferred_element_type=F32) for v in (high, low))


def mix_local(place, value):
    for index in range(place.others):
        k = place.col_bits - 1 - index
        s = sign_of(place.tok[place.extra + k])
        own = lax.index_in_dim(value, 0, index, keepdims=True)
        got = lax.index_in_dim(value, 1, index, keepdims=True)
        value = jnp.concatenate([own + got, s * (own - got)], axis=index)
    width = value.shape[-1]
    value = value.reshape(-1, place.fine, width)
    value = times_table(value, hadamard(width), False)
    value = times_table(value, hadamard(place.fine), True)
    return value.reshape(place.rows, width)


def body(activations, out_grads, token_mask, row_signs, col_signs, bank, bank_index):
    seqs, tokens, block = activations.shape
    width = block * lax.axis_size("col")
    rows = row_signs.shape[0]
    place = Place(width, rows, block)
    col_pm = (2 * col_signs - 1).astype(BF16)
    squared = float(width) * float(width)
    slots = max(16, (tokens * 13 // 16) // 16 * 16)

    order = jnp.arange(tokens, dtype=jnp.int32)
    earlier = (order[None, :] <= order[:, None]).astype(jnp.int32)
    rank = jnp.sum(earlier[None] * token_mask[:, None, :], axis=-1) - 1
    counts = jnp.sum(token_mask, axis=-1)
    target = jnp.where(token_mask > 0, rank, -1)

    def compact(seq_number, start, count):
        wanted = start + jnp.arange(count, dtype=jnp.int32)
        pick = (target[seq_number][None, :] == wanted[:, None]).astype(BF16)
        a = jnp.dot(pick, activations[seq_number], preferred_element_type=BF16)
        m = jnp.dot(pick, out_grads[seq_number], preferred_element_type=BF16) * col_pm[None, :]
        return a, m

    note = jnp.broadcast_to(jnp.max(counts), (128,)).astype(jnp.int32)
    gathered = lax.all_gather(jnp.concatenate([row_signs, note]), "tok", axis=0)
    row_pm = (2 * gathered[:, :rows] - 1).astype(F32).reshape(-1)
    overflow = jnp.max(gathered[:, rows]) > slots

    packed = [compact(s, 0, slots) for s in range(seqs)]
    slabs = pipeline(place, [p[0] for p in packed], [p[1] for p in packed], row_pm, (1,) * (seqs - 1) + (2,))

    def with_rest(slabs):
        rest = [compact(s, slots, tokens - slots) for s in range(seqs)]
        more = pipeline(place, [p[0] for p in rest], [p[1] for p in rest], row_pm, (1,) * seqs)
        return [a + b for a, b in zip(slabs, more)]

    slabs = lax.cond(overflow, with_rest, lambda v: v, slabs)

    prints, sums = [], []
    for seq_number in range(seqs):
        finished = mix_local(place, slabs[seq_number]) * (1.0 / width)
        chosen = lax.dynamic_index_in_dim(bank, bank_index[seq_number], 0, keepdims=False)
        prints.append(finished)
        sums.append(jnp.stack([
            jnp.sum(finished * chosen), jnp.sum(finished * finished), jnp.sum(chosen * chosen)
        ]))
    total = jnp.stack(sums)
    for axis in ("tok", "col"):
        for k in range(bits_of(lax.axis_size(axis))):
            total = total + swap(total, axis, 1 << k)
    cross, own, refsq = total[:, 0], total[:, 1], total[:, 2]
    scores = width * (cross / squared) / jnp.sqrt((own / squared + 1e-06) * (refsq / squared + 1e-06))
    return (jnp.stack(prints), scores)


def solution(mesh):
    in_specs = (
        P(None, "tok", "col"),
        P(None, "tok", "col"),
        P(None, "tok"),
        P("tok"),
        P("col"),
        P(None, "tok", "col"),
        P(),
    )
    out_specs = (P(None, "tok", "col"), P())
    return jax.shard_map(body, mesh=mesh, in_specs=in_specs, out_specs=out_specs, check_vma=False)
```
